32 devices in a mesh: parts: 2 (over y), clip: 4 (over x, core), tensor: 4 (over z).
Axes of the slice: x: 2, y: 2, z: 4, core: 2. Of those that a mesh axis runs over, the one named last changes fastest.
Arguments:
- clips: bfloat16 [32, 128, 4096], P(('parts', 'clip'), None, 'tensor'), parts along dimension 0, may hold values from -6 to 6
- targets: bfloat16 [32, 128, 4096], P(('parts', 'clip'), None, 'tensor'), parts along dimension 0, may hold values from -6 to 6
- lengths: int32 [32], P(('parts', 'clip')), parts along dimension 0, may hold values from 32 to 128, as said below
- gate_weight: bfloat16 [4096, 7168], P(None, 'tensor'), may hold values from -0.09375 to 0.09375
- up_weight: bfloat16 [4096, 7168], P(None, 'tensor'), may hold values from -0.09375 to 0.09375
- down_weight: bfloat16 [7168, 4096], P('tensor'), may hold values from -0.0625 to 0.0625
- proj_in: bfloat16 [64, 7168], P(None, 'tensor'), may hold values from -0.0625 to 0.0625
- proj_out: bfloat16 [64, 4096], replicated, may hold values from -0.09375 to 0.09375
- inv_hessian: bfloat16 [4096, 4096], P('clip', 'tensor'), may hold values from -0.2 to 2.2, as said below
- test_sketches: bfloat16 [4096, 4096], P('clip', 'tensor'), may hold values from -6 to 6
Outputs:
- scores: float32 [32, 4096], P(('parts', 'clip'), 'tensor'), parts along dimension 0
The draws below stay inside these ranges and needn't reach their ends.
There are 2 independent parts, one for each index of `parts`. The reference program is written for one: setup_inputs(seed, part) draws one part's arguments, and reference() takes and returns one part's arrays. A program takes and returns all parts, laid end to end along the dimension named above; an argument that names none is the same for every part. Nothing has to cross between parts.
Inputs may be any that keep to these rules, and one draw needn't show every extreme that they name: `lengths`: every clip has between 32 and 128 valid tokens; in each part one clip has exactly 128 and another exactly 32. `inv_hessian`: the same matrix in both parts.
All inputs are finite; a program needn't handle non-finite values.
Results may differ from the reference program's by a relative error of at most 0.0066.
Values may be sent and summed in bfloat16 or wider, within the bound.
A program may use at most 192 MiB of HBM per device.

```python
import math
import jax
import jax.numpy as jnp
from jax import lax

D = 4096
FF = 7168
PROJ = 64
FEAT = 4096
NTEST = 4096
LEN = 128
CLIPS = 16


def draw_lengths(key, part):
    first_key, second_key = jax.random.split(key)
    counts = jax.random.randint(first_key, (CLIPS,), LEN // 4, LEN + 1)
    chosen = jax.random.randint(second_key, (), 0, CLIPS)
    places = jnp.arange(CLIPS)
    counts = jnp.where(places == chosen, LEN, counts)
    counts = jnp.where(places == (chosen + 1) % CLIPS, LEN // 4, counts)
    return counts.astype(jnp.int32)


def draw_inv_hessian(key, part):
    first_key, second_key = jax.random.split(key)
    spread = jax.random.truncated_normal(first_key, -5.0, 5.0, (FEAT, FEAT), jnp.float32) * 0.02
    diag_vals = jnp.exp(jax.random.uniform(second_key, (FEAT,), jnp.float32, math.log(0.5), math.log(2.0)))
    places = jnp.arange(FEAT)
    on_diag = places[:, None] == places[None, :]
    return jnp.where(on_diag, diag_vals[None, :], spread).astype(jnp.bfloat16)


def block_scale(own_key, dims, cuts, smallest, high):
    gain = 1.0
    for dim, parts in cuts:
        steps = jax.random.uniform(jax.random.fold_in(jax.random.fold_in(own_key, 6), dim), (parts,), jnp.float32, smallest / len(cuts), high / len(cuts))
        gain = gain * jnp.repeat(jnp.exp(steps), dims[dim] // parts).reshape((-1,) + (1,) * (len(dims) - 1 - dim))
    return gain


def centred(stream_key, shape, scale, most, cuts=(), kind=jnp.bfloat16):
    array = jax.random.normal(stream_key, shape, jnp.float32) * scale
    if len(cuts) > 0:
        array = block_scale(stream_key, shape, cuts, -0.22, 0.18) * array
    return jnp.clip(array, min=-most, max=most).astype(kind)


def setup_inputs(seed: int = 0, part: int = 0) -> dict:
    keys = jax.random.split(jax.random.key(seed), 11)
    own_keys = jax.random.split(jax.random.fold_in(keys[10], part), 11)
    return {
        "clips": centred(own_keys[0], (CLIPS, LEN, D), 1.0, 6.0, ((0, 4), (2, 4))),
        "targets": centred(own_keys[1], (CLIPS, LEN, D), 1.0, 6.0, ((0, 4), (2, 4))),
        "lengths": draw_lengths(jax.random.fold_in(jax.random.fold_in(keys[10], part), 71), part),
        "gate_weight": centred(keys[3], (D, FF), D ** -0.5, 0.09375, ((1, 4),)),
        "up_weight": centred(keys[4], (D, FF), D ** -0.5, 0.09375, ((1, 4),)),
        "down_weight": centred(keys[5], (FF, D), FF ** -0.5, 0.0625, ((0, 4),)),
        "proj_in": centred(keys[6], (PROJ, FF), FF ** -0.5, 0.0625, ((1, 4),)),
        "proj_out": centred(keys[7], (PROJ, D), D ** -0.5, 0.09375),
        "inv_hessian": draw_inv_hessian(jax.random.fold_in(keys[10], 71), part),
        "test_sketches": centred(keys[9], (NTEST, FEAT), 1.0, 6.0, ((0, 4), (1, 4))),
    }


def reference(clips, targets, lengths, gate_weight, up_weight, down_weight, proj_in, proj_out, inv_hessian, test_sketches):
    def one_clip(items):
        tokens, golden, valid = items
        gate = jnp.dot(tokens, gate_weight, preferred_element_type=jnp.float32)
        upward = jnp.dot(tokens, up_weight, preferred_element_type=jnp.float32)
        hidden = (jax.nn.silu(gate) * upward).astype(jnp.bfloat16)
        output = jnp.dot(hidden, down_weight, preferred_element_type=jnp.float32)
        position = jnp.arange(LEN, dtype=jnp.int32)
        weight = jnp.where(position < valid, 1.0, 0.0).astype(jnp.float32) / valid.astype(jnp.float32)
        differ = jnp.clip(output - golden.astype(jnp.float32), -1.0, 1.0)
        grad_out = (differ * weight[:, None]).astype(jnp.bfloat16)
        left = jnp.dot(hidden, proj_in.T, preferred_element_type=jnp.float32)
        right = jnp.dot(grad_out, proj_out.T, preferred_element_type=jnp.float32)
        sketch = jnp.dot(left.T, right, precision=lax.Precision.HIGHEST)
        return sketch.reshape(FEAT)

    sketches = lax.map(one_clip, (clips, targets, lengths)).astype(jnp.bfloat16)
    precond = jnp.dot(sketches, inv_hessian, preferred_element_type=jnp.float32).astype(jnp.bfloat16)
    return jnp.dot(precond, test_sketches.T, preferred_element_type=jnp.float32)
```

```python
import functools

import jax
import jax.numpy as jnp
from jax import lax
from jax.experimental import pallas as pl
from jax.experimental.pallas import tpu as pltpu
from jax.sharding import PartitionSpec as P

MESH = pl.DeviceIdType.MESH


def entry_barrier(n, me):
    barrier = pltpu.get_barrier_semaphore()

    @pl.loop(0, n)
    def _(j):
        @pl.when(j != me)
        def _():
            pl.semaphore_signal(barrier, inc=1, device_id={"tensor": j}, device_id_type=MESH)

    pl.semaphore_wait(barrier, n - 1)


def layer_kernel(
    n,
    tile,
    clips_ref,
    targets_ref,
    weight_ref,
    gate_hbm,
    up_hbm,
    down_hbm,
    pin_ref,
    pout_ref,
    sketch_ref,
    gate_ref,
    up_ref,
    down_ref,
    tok,
    slots,
    hid,
    joined,
    parts,
    gathered,
    load_sem,
    ag_send,
    ag_recv,
    rs_send,
    rs_recv,
    own_send,
    own_recv,
    sk_send,
    sk_recv,
):
    me = lax.axis_index("tensor")
    count, rows, width = targets_ref.shape
    hidden_part = gate_ref.shape[1]
    last = n - 1
    tile_w = 256 if width % 256 == 0 else width

    own = pltpu.make_async_copy(clips_ref, tok.at[:, me], load_sem.at[0])
    own.start()
    loads = [
        pltpu.make_async_copy(gate_hbm, gate_ref, load_sem.at[1]),
        pltpu.make_async_copy(up_hbm, up_ref, load_sem.at[2]),
        pltpu.make_async_copy(down_hbm, down_ref, load_sem.at[3]),
    ]
    entry_barrier(n, me)
    own.wait()

    def token_copy(side, k, j):
        target = me + 1 if side == 0 else me - 1
        return pltpu.make_async_remote_copy(
            src_ref=tok.at[k, j],
            dst_ref=tok.at[k, j],
            send_sem=ag_send.at[side, k, j],
            recv_sem=ag_recv.at[k, j],
            device_id={"tensor": target},
            device_id_type=MESH,
        )

    def sum_copy(side, k, d):
        if side == 0:
            target, slot = me + 1, d
        else:
            target = me - 1
            slot = jnp.where(d == me - 1, n, d)
        return pltpu.make_async_remote_copy(
            src_ref=slots.at[k, d],
            dst_ref=slots.at[k, slot],
            send_sem=rs_send.at[k, d],
            recv_sem=rs_recv.at[k, slot],
            device_id={"tensor": target},
            device_id_type=MESH,
        )

    def wait_slot(k, slot):
        pltpu.make_async_copy(slots.at[k, slot], slots.at[k, slot], rs_recv.at[k, slot]).wait()

    def wait_token(k, j):
        pltpu.make_async_copy(tok.at[k, j], tok.at[k, j], ag_recv.at[k, j]).wait()

    def partial_tile(k, d, t):
        start = pl.multiple_of(d * width + t * tile_w, tile_w)
        return jnp.dot(
            hid[k], down_ref[:, pl.ds(start, tile_w)], preferred_element_type=jnp.float32
        )

    def add_and_send(side, k, d):
        first = me == (0 if side == 0 else last)

        @pl.when(first)
        def _():
            @pl.loop(0, width // tile_w)
            def _(t):
                cols = pl.ds(pl.multiple_of(t * tile_w, tile_w), tile_w)
                slots[k, d, :, cols] = partial_tile(k, d, t).astype(jnp.bfloat16)

        @pl.when(jnp.logical_not(first))
        def _():
            wait_slot(k, d)

            @pl.loop(0, width // tile_w)
            def _(t):
                cols = pl.ds(pl.multiple_of(t * tile_w, tile_w), tile_w)
                got = slots[k, d, :, cols].astype(jnp.float32)
                slots[k, d, :, cols] = (partial_tile(k, d, t) + got).astype(jnp.bfloat16)

        sum_copy(side, k, d).start()

    def forward_hidden(k):
        @pl.loop(0, hidden_part // tile)
        def _(t):
            cols = pl.ds(pl.multiple_of(t * tile, tile), tile)
            gate_act = jnp.zeros((rows, tile), jnp.float32)
            up_act = jnp.zeros((rows, tile), jnp.float32)
            for j in range(n):
                piece = tok[k, j]
                gate_act += jnp.dot(
                    piece,
                    gate_ref[j * width : (j + 1) * width, cols],
                    preferred_element_type=jnp.float32,
                )
                up_act += jnp.dot(
                    piece,
                    up_ref[j * width : (j + 1) * width, cols],
                    preferred_element_type=jnp.float32,
                )
            silu = gate_act / (1.0 + jnp.exp(-gate_act))
            hid[k, :, cols] = (silu * up_act).astype(jnp.bfloat16)

        joined[k] = jnp.dot(hid[k], pin_ref[...], preferred_element_type=jnp.float32)

    def finish(k):
        @pl.when(me > 0)
        def _():
            wait_slot(k, me)

        @pl.when(me < last)
        def _():
            wait_slot(k, n)

        from_left = jnp.where(me > 0, 1.0, 0.0)
        from_right = jnp.where(me < last, 1.0, 0.0)
        has_left = jnp.full((rows, tile_w), from_left, jnp.float32) > 0.5
        has_right = jnp.full((rows, tile_w), from_right, jnp.float32) > 0.5

        @pl.loop(0, width // tile_w)
        def _(t):
            cols = pl.ds(pl.multiple_of(t * tile_w, tile_w), tile_w)
            total = partial_tile(k, me, t)
            total += jnp.where(has_left, slots[k, me, :, cols].astype(jnp.float32), 0.0)
            total += jnp.where(has_right, slots[k, n, :, cols].astype(jnp.float32), 0.0)
            differ = jnp.clip(total - targets_ref[k, :, cols].astype(jnp.float32), -1.0, 1.0)
            grad = (differ * weight_ref[k]).astype(jnp.bfloat16)
            joined[k] += jnp.dot(
                grad, pout_ref[cols, :], preferred_element_type=jnp.float32
            )

        @pl.when(me != k)
        def _():
            part_copy(k).start()

    def part_copy(k):
        return pltpu.make_async_remote_copy(
            src_ref=joined.at[k],
            dst_ref=parts.at[me],
            send_sem=own_send.at[k],
            recv_sem=own_recv.at[me],
            device_id={"tensor": k},
            device_id_type=MESH,
        )

    def sketch_copy(j):
        return pltpu.make_async_remote_copy(
            src_ref=gathered.at[me],
            dst_ref=gathered.at[me],
            send_sem=sk_send.at[j],
            recv_sem=sk_recv.at[me],
            device_id={"tensor": j},
            device_id_type=MESH,
        )

    @pl.loop(0, count + 2 * last)
    def _(step):
        @pl.when(step < count)
        def _():
            @pl.when(me < last)
            def _():
                token_copy(0, step, me).start()

            @pl.when(me > 0)
            def _():
                token_copy(1, step, me).start()

        @pl.when(step == 0)
        def _():
            for load in loads:
                load.start()

        @pl.loop(1, n)
        def _(h):
            k = step - h

            @pl.when((k >= 0) & (k < count))
            def _():
                @pl.when(me - h >= 0)
                def _():
                    wait_token(k, me - h)

                    @pl.when(me < last)
                    def _():
                        token_copy(0, k, me - h).start()

                @pl.when(me + h <= last)
                def _():
                    wait_token(k, me + h)

                    @pl.when(me > 0)
                    def _():
                        token_copy(1, k, me + h).start()

        @pl.when(step == last)
        def _():
            for load in loads:
                load.wait()

        k_now = step - last

        @pl.when((k_now >= 0) & (k_now < count))
        def _():
            forward_hidden(k_now)

        k_right = step - last - me

        @pl.when((k_right >= 0) & (k_right < count))
        def _():
            @pl.loop(0, last - me)
            def _(i):
                add_and_send(0, k_right, last - i)

        k_left = step - last - (last - me)

        @pl.when((k_left >= 0) & (k_left < count))
        def _():
            @pl.loop(0, me)
            def _(d):
                add_and_send(1, k_left, d)

        k_end = step - 2 * last

        @pl.when((k_end >= 0) & (k_end < count))
        def _():
            finish(k_end)

    @pl.when(me < count)
    def _():
        total = joined[me]
        parts[me] = total

        @pl.loop(0, n)
        def _(j):
            @pl.when(j != me)
            def _():
                pltpu.make_async_copy(parts.at[j], parts.at[j], own_recv.at[j]).wait()

        total = parts[0]
        for j in range(1, n):
            total += parts[j]
        product = jnp.dot(
            total.T,
            total,
            precision=lax.Precision.HIGHEST,
            preferred_element_type=jnp.float32,
        )
        gathered[me] = product.astype(jnp.bfloat16)

        @pl.loop(0, n)
        def _(j):
            @pl.when(j != me)
            def _():
                sketch_copy(j).start()

    @pl.loop(0, count)
    def _(k):
        @pl.when(k != me)
        def _():
            pltpu.make_async_copy(gathered.at[k], gathered.at[k], sk_recv.at[k]).wait()

    sketch_ref[...] = gathered[...]

    @pl.when(me < count)
    def _():
        @pl.loop(0, n)
        def _(j):
            @pl.when(j != me)
            def _():
                sketch_copy(j).wait_send()

    @pl.loop(0, count)
    def _(k):
        @pl.when(k != me)
        def _():
            part_copy(k).wait_send()

        @pl.loop(0, n)
        def _(j):
            @pl.when((j <= me) & (me < last))
            def _():
                token_copy(0, k, j).wait_send()

            @pl.when((j >= me) & (me > 0))
            def _():
                token_copy(1, k, j).wait_send()

            @pl.when(j > me)
            def _():
                sum_copy(0, k, j).wait_send()

            @pl.when(j < me)
            def _():
                sum_copy(1, k, j).wait_send()


def scatter_kernel(n, x_ref, out_ref, pieces, send_sem, recv_sem, landed):
    me = lax.axis_index("tensor")
    width = out_ref.shape[1]
    for j in range(n):
        pieces[j] = x_ref[:, j * width : (j + 1) * width]
    entry_barrier(n, me)

    def copy(j):
        return pltpu.make_async_remote_copy(
            src_ref=pieces.at[j],
            dst_ref=landed.at[me],
            send_sem=send_sem.at[j],
            recv_sem=recv_sem.at[me],
            device_id={"tensor": j},
            device_id_type=MESH,
        )

    @pl.loop(0, n)
    def _(j):
        @pl.when(j != me)
        def _():
            copy(j).start()

    landed[me] = pieces[me]

    @pl.loop(0, n)
    def _(j):
        @pl.when(j != me)
        def _():
            pltpu.make_async_copy(landed.at[j], landed.at[j], recv_sem.at[j]).wait()

    total = landed[0]
    for j in range(1, n):
        total += landed[j]
    out_ref[...] = total

    @pl.loop(0, n)
    def _(j):
        @pl.when(j != me)
        def _():
            copy(j).wait_send()


def on_device(
    n,
    clips,
    targets,
    lengths,
    gate_weight,
    up_weight,
    down_weight,
    proj_in,
    proj_out,
    inv_hessian,
    test_sketches,
):
    count, rows, width = clips.shape
    hidden_part = gate_weight.shape[1]
    proj_size = proj_in.shape[0]
    full_hessian = lax.all_gather(inv_hessian, "clip", axis=0, tiled=True)
    full_tests = lax.all_gather(test_sketches, "clip", axis=0, tiled=True)

    position = jnp.arange(rows, dtype=jnp.int32)
    valid = (position[None, :] < lengths[:, None]).astype(jnp.float32)
    weight = (valid / lengths.astype(jnp.float32)[:, None])[:, :, None]
    start = lax.axis_index("tensor") * width
    proj_cols = lax.dynamic_slice_in_dim(proj_out, start, width, 1)
    pin = jnp.pad(proj_in.T, ((0, 0), (0, proj_size)))
    pout = jnp.pad(proj_cols.T, ((0, 0), (proj_size, 0)))
    both = 2 * proj_size

    tile = 256 if hidden_part % 256 == 0 else hidden_part
    vmem = pl.BlockSpec(memory_space=pltpu.VMEM)
    hbm = pl.BlockSpec(memory_space=pltpu.HBM)
    bf16, f32 = jnp.bfloat16, jnp.float32
    dma = pltpu.SemaphoreType.DMA
    sketches = pl.pallas_call(
        functools.partial(layer_kernel, n, tile),
        out_shape=jax.ShapeDtypeStruct((count, both, both), bf16),
        in_specs=[hbm, vmem, vmem, hbm, hbm, hbm, vmem, vmem],
        out_specs=vmem,
        scratch_shapes=[
            pltpu.VMEM(gate_weight.shape, bf16),
            pltpu.VMEM(up_weight.shape, bf16),
            pltpu.VMEM(down_weight.shape, bf16),
            pltpu.VMEM((count, n, rows, width), bf16),
            pltpu.VMEM((count, n + 1, rows, width), bf16),
            pltpu.VMEM((count, rows, hidden_part), bf16),
            pltpu.VMEM((count, rows, both), f32),
            pltpu.VMEM((n, rows, both), f32),
            pltpu.VMEM((count, both, both), bf16),
            dma((4,)),
            dma((2, count, n)),
            dma((count, n)),
            dma((count, n)),
            dma((count, n + 1)),
            dma((count,)),
            dma((n,)),
            dma((n,)),
            dma((count,)),
        ],
        compiler_params=pltpu.CompilerParams(
            collective_id=0, has_side_effects=True, vmem_limit_bytes=62 * 1024 * 1024
        ),
        cost_estimate=pl.CostEstimate(
            flops=6 * count * rows * hidden_part * width * n,
            bytes_accessed=400_000_000,
            transcendentals=count * rows * hidden_part,
        ),
        name="layer",
    )(clips, targets, weight, gate_weight, up_weight, down_weight, pin, pout)

    flat_sketch = sketches[:, :proj_size, proj_size:].reshape(count, proj_size * proj_size)
    precond = jnp.dot(
        flat_sketch, full_hessian, preferred_element_type=jnp.float32
    ).astype(jnp.bfloat16)
    partial_scores = lax.dot_general(
        precond,
        full_tests,
        (((1,), (1,)), ((), ())),
        preferred_element_type=jnp.float32,
    )
    out_width = partial_scores.shape[1] // n
    return pl.pallas_call(
        functools.partial(scatter_kernel, n),
        out_shape=jax.ShapeDtypeStruct((count, out_width), f32),
        in_specs=[vmem],
        out_specs=vmem,
        scratch_shapes=[
            pltpu.VMEM((n, count, out_width), f32),
            dma((n,)),
            dma((n,)),
            pltpu.VMEM((n, count, out_width), f32),
        ],
        compiler_params=pltpu.CompilerParams(collective_id=1, has_side_effects=True),
        name="scatter",
    )(partial_scores)


def solution(mesh):
    in_specs = (
        P(("parts", "clip"), None, "tensor"),
        P(("parts", "clip"), None, "tensor"),
        P(("parts", "clip")),
        P(None, "tensor"),
        P(None, "tensor"),
        P("tensor", None),
        P(None, "tensor"),
        P(),
        P("clip", "tensor"),
        P("clip", "tensor"),
    )
    out_specs = P(("parts", "clip"), "tensor")
    return jax.shard_map(
        functools.partial(on_device, mesh.shape["tensor"]),
        mesh=mesh,
        in_specs=in_specs,
        out_specs=out_specs,
        check_vma=False,
    )
```

```python
import functools

import jax
import jax.numpy as jnp
from jax import lax
from jax.experimental import pallas as pl
from jax.experimental.pallas import tpu as pltpu
from jax.sharding import PartitionSpec as P

MESH = pl.DeviceIdType.MESH


def entry_barrier(n, me):
    barrier = pltpu.get_barrier_semaphore()

    @pl.loop(0, n)
    def _(j):
        @pl.when(j != me)
        def _():
            pl.semaphore_signal(barrier, inc=1, device_id={"tensor": j}, device_id_type=MESH)

    pl.semaphore_wait(barrier, n - 1)


def layer_kernel(
    n,
    tile,
    clips_ref,
    targets_ref,
    weight_ref,
    gate_hbm,
    up_hbm,
    down_hbm,
    pin_ref,
    pout_ref,
    sketch_ref,
    gate_ref,
    up_ref,
    down_ref,
    tok,
    slots,
    hid,
    joined,
    parts,
    gathered,
    load_sem,
    ag_send,
    ag_recv,
    rs_send,
    rs_recv,
    own_send,
    own_recv,
    sk_send,
    sk_recv,
):
    me = lax.axis_index("tensor")
    count, rows, width = targets_ref.shape
    hidden_part = gate_ref.shape[1]
    last = n - 1
    tile_w = 256 if width % 256 == 0 else width

    own = pltpu.make_async_copy(clips_ref, tok.at[:, me], load_sem.at[0])
    own.start()
    loads = [
        pltpu.make_async_copy(gate_hbm, gate_ref, load_sem.at[1]),
        pltpu.make_async_copy(up_hbm, up_ref, load_sem.at[2]),
        pltpu.make_async_copy(down_hbm, down_ref, load_sem.at[3]),
    ]
    entry_barrier(n, me)
    own.wait()

    def token_copy(side, k, j):
        target = me + 1 if side == 0 else me - 1
        return pltpu.make_async_remote_copy(
            src_ref=tok.at[k, j],
            dst_ref=tok.at[k, j],
            send_sem=ag_send.at[side, k, j],
            recv_sem=ag_recv.at[k, j],
            device_id={"tensor": target},
            device_id_type=MESH,
        )

    def sum_copy(side, k, d):
        if side == 0:
            target, slot = me + 1, d
        else:
            target = me - 1
            slot = jnp.where(d == me - 1, n, d)
        return pltpu.make_async_remote_copy(
            src_ref=slots.at[k, d],
            dst_ref=slots.at[k, slot],
            send_sem=rs_send.at[k, d],
            recv_sem=rs_recv.at[k, slot],
            device_id={"tensor": target},
            device_id_type=MESH,
        )

    def wait_slot(k, slot):
        pltpu.make_async_copy(slots.at[k, slot], slots.at[k, slot], rs_recv.at[k, slot]).wait()

    def wait_token(k, j):
        pltpu.make_async_copy(tok.at[k, j], tok.at[k, j], ag_recv.at[k, j]).wait()

    def partial_tile(k, d, t):
        start = pl.multiple_of(d * width + t * tile_w, tile_w)
        return jnp.dot(
            hid[k], down_ref[:, pl.ds(start, tile_w)], preferred_element_type=jnp.float32
        )

    def add_and_send(side, k, d):
        first = me == (0 if side == 0 else last)

        @pl.when(first)
        def _():
            @pl.loop(0, width // tile_w)
            def _(t):
                cols = pl.ds(pl.multiple_of(t * tile_w, tile_w), tile_w)
                slots[k, d, :, cols] = partial_tile(k, d, t).astype(jnp.bfloat16)

        @pl.when(jnp.logical_not(first))
        def _():
            wait_slot(k, d)

            @pl.loop(0, width // tile_w)
            def _(t):
                cols = pl.ds(pl.multiple_of(t * tile_w, tile_w), tile_w)
                got = slots[k, d, :, cols].astype(jnp.float32)
                slots[k, d, :, cols] = (partial_tile(k, d, t) + got).astype(jnp.bfloat16)

        sum_copy(side, k, d).start()

    def forward_hidden(k):
        @pl.loop(0, hidden_part // tile)
        def _(t):
            cols = pl.ds(pl.multiple_of(t * tile, tile), tile)
            gate_act = jnp.zeros((rows, tile), jnp.float32)
            up_act = jnp.zeros((rows, tile), jnp.float32)
            for j in range(n):
                piece = tok[k, j]
                gate_act += jnp.dot(
                    piece,
                    gate_ref[j * width : (j + 1) * width, cols],
                    preferred_element_type=jnp.float32,
                )
                up_act += jnp.dot(
                    piece,
                    up_ref[j * width : (j + 1) * width, cols],
                    preferred_element_type=jnp.float32,
                )
            silu = gate_act / (1.0 + jnp.exp(-gate_act))
            hid[k, :, cols] = (silu * up_act).astype(jnp.bfloat16)

        joined[k] = jnp.dot(hid[k], pin_ref[...], preferred_element_type=jnp.float32)

    def finish(k):
        @pl.when(me > 0)
        def _():
            wait_slot(k, me)

        @pl.when(me < last)
        def _():
            wait_slot(k, n)

        from_left = jnp.where(me > 0, 1.0, 0.0)
        from_right = jnp.where(me < last, 1.0, 0.0)
        has_left = jnp.full((rows, tile_w), from_left, jnp.float32) > 0.5
        has_right = jnp.full((rows, tile_w), from_right, jnp.float32) > 0.5

        @pl.loop(0, width // tile_w)
        def _(t):
            cols = pl.ds(pl.multiple_of(t * tile_w, tile_w), tile_w)
            total = partial_tile(k, me, t)
            total += jnp.where(has_left, slots[k, me, :, cols].astype(jnp.float32), 0.0)
            total += jnp.where(has_right, slots[k, n, :, cols].astype(jnp.float32), 0.0)
            differ = jnp.clip(total - targets_ref[k, :, cols].astype(jnp.float32), -1.0, 1.0)
            grad = (differ * weight_ref[k]).astype(jnp.bfloat16)
            joined[k] += jnp.dot(
                grad, pout_ref[cols, :], preferred_element_type=jnp.float32
            )

        @pl.when(me != k)
        def _():
            part_copy(k).start()

    def part_copy(k):
        return pltpu.make_async_remote_copy(
            src_ref=joined.at[k],
            dst_ref=parts.at[me],
            send_sem=own_send.at[k],
            recv_sem=own_recv.at[me],
            device_id={"tensor": k},
            device_id_type=MESH,
        )

    def sketch_copy(j):
        return pltpu.make_async_remote_copy(
            src_ref=gathered.at[me],
            dst_ref=gathered.at[me],
            send_sem=sk_send.at[j],
            recv_sem=sk_recv.at[me],
            device_id={"tensor": j},
            device_id_type=MESH,
        )

    @pl.loop(0, count + 2 * last)
    def _(step):
        @pl.when(step < count)
        def _():
            @pl.when(me < last)
            def _():
                token_copy(0, step, me).start()

            @pl.when(me > 0)
            def _():
                token_copy(1, step, me).start()

        @pl.when(step == 0)
        def _():
            for load in loads:
                load.start()

        @pl.loop(1, n)
        def _(h):
            k = step - h

            @pl.when((k >= 0) & (k < count))
            def _():
                @pl.when(me - h >= 0)
                def _():
                    wait_token(k, me - h)

                    @pl.when(me < last)
                    def _():
                        token_copy(0, k, me - h).start()

                @pl.when(me + h <= last)
                def _():
                    wait_token(k, me + h)

                    @pl.when(me > 0)
                    def _():
                        token_copy(1, k, me + h).start()

        @pl.when(step == last)
        def _():
            for load in loads:
                load.wait()

        k_now = step - last

        @pl.when((k_now >= 0) & (k_now < count))
        def _():
            forward_hidden(k_now)

        k_right = step - last - me

        @pl.when((k_right >= 0) & (k_right < count))
        def _():
            @pl.loop(0, last - me)
            def _(i):
                add_and_send(0, k_right, last - i)

        k_left = step - last - (last - me)

        @pl.when((k_left >= 0) & (k_left < count))
        def _():
            @pl.loop(0, me)
            def _(d):
                add_and_send(1, k_left, d)

        k_end = step - 2 * last

        @pl.when((k_end >= 0) & (k_end < count))
        def _():
            finish(k_end)

    @pl.when(me < count)
    def _():
        total = joined[me]
        parts[me] = total

        @pl.loop(0, n)
        def _(j):
            @pl.when(j != me)
            def _():
                pltpu.make_async_copy(parts.at[j], parts.at[j], own_recv.at[j]).wait()

        total = parts[0]
        for j in range(1, n):
            total += parts[j]
        product = jnp.dot(
            total.T,
            total,
            precision=lax.Precision.HIGHEST,
            preferred_element_type=jnp.float32,
        )
        gathered[me] = product.astype(jnp.bfloat16)

        @pl.loop(0, n)
        def _(j):
            @pl.when(j != me)
            def _():
                sketch_copy(j).start()

    @pl.loop(0, count)
    def _(k):
        @pl.when(k != me)
        def _():
            pltpu.make_async_copy(gathered.at[k], gathered.at[k], sk_recv.at[k]).wait()

    sketch_ref[...] = gathered[...]

    @pl.when(me < count)
    def _():
        @pl.loop(0, n)
        def _(j):
            @pl.when(j != me)
            def _():
                sketch_copy(j).wait_send()

    @pl.loop(0, count)
    def _(k):
        @pl.when(k != me)
        def _():
            part_copy(k).wait_send()

        @pl.loop(0, n)
        def _(j):
            @pl.when((j <= me) & (me < last))
            def _():
                token_copy(0, k, j).wait_send()

            @pl.when((j >= me) & (me > 0))
            def _():
                token_copy(1, k, j).wait_send()

            @pl.when(j > me)
            def _():
                sum_copy(0, k, j).wait_send()

            @pl.when(j < me)
            def _():
                sum_copy(1, k, j).wait_send()


def score_kernel(
    nc,
    n,
    flat_ref,
    hessian_ref,
    tests_ref,
    out_ref,
    pieces,
    landed_pieces,
    stacked,
    partial,
    landed_partial,
    blocks,
    landed_blocks,
    send_a,
    recv_a,
    send_b,
    recv_b,
    send_c,
    recv_c,
):
    my_clip = lax.axis_index("clip")
    me = lax.axis_index("tensor")
    count, out_width = out_ref.shape
    depth = hessian_ref.shape[0]
    ratio = n // nc

    barrier = pltpu.get_barrier_semaphore()

    @pl.loop(0, nc)
    def _(c):
        @pl.loop(0, n)
        def _(z):
            @pl.when((c != my_clip) | (z != me))
            def _():
                pl.semaphore_signal(
                    barrier, inc=1, device_id={"clip": c, "tensor": z}, device_id_type=MESH
                )

    for c in range(nc):
        pieces[c] = flat_ref[:, c * depth : (c + 1) * depth].astype(jnp.float32)
    pl.semaphore_wait(barrier, nc * n - 1)

    def piece_copy(c):
        return pltpu.make_async_remote_copy(
            src_ref=pieces.at[c],
            dst_ref=landed_pieces.at[my_clip],
            send_sem=send_a.at[c],
            recv_sem=recv_a.at[my_clip],
            device_id={"clip": c, "tensor": me},
            device_id_type=MESH,
        )

    def partial_copy(c):
        return pltpu.make_async_remote_copy(
            src_ref=partial,
            dst_ref=landed_partial.at[my_clip],
            send_sem=send_b.at[c],
            recv_sem=recv_b.at[my_clip],
            device_id={"clip": c, "tensor": me},
            device_id_type=MESH,
        )

    def block_copy(c, q):
        return pltpu.make_async_remote_copy(
            src_ref=blocks.at[c, q],
            dst_ref=landed_blocks.at[me],
            send_sem=send_c.at[c, q],
            recv_sem=recv_c.at[me],
            device_id={"clip": c, "tensor": my_clip * ratio + q},
            device_id_type=MESH,
        )

    def other_clips(act):
        @pl.loop(0, nc)
        def _(c):
            @pl.when(c != my_clip)
            def _():
                act(c)

    def wait_for(ref, sem):
        pltpu.make_async_copy(ref, ref, sem).wait()

    other_clips(lambda c: piece_copy(c).start())
    landed_pieces[my_clip] = pieces[my_clip]
    other_clips(lambda c: wait_for(landed_pieces.at[c], recv_a.at[c]))
    for c in range(nc):
        stacked[c * count : (c + 1) * count, :] = landed_pieces[c]
    partial[...] = jnp.dot(
        stacked[...].astype(jnp.bfloat16),
        hessian_ref[...],
        preferred_element_type=jnp.float32,
    )
    other_clips(lambda c: partial_copy(c).start())
    landed_partial[my_clip] = partial[...]
    other_clips(lambda c: wait_for(landed_partial.at[c], recv_b.at[c]))
    precond = landed_partial[0]
    for c in range(1, nc):
        precond += landed_partial[c]
    scores = lax.dot_general(
        precond.astype(jnp.bfloat16),
        tests_ref[...],
        (((1,), (1,)), ((), ())),
        preferred_element_type=jnp.float32,
    )
    for c in range(nc):
        for q in range(ratio):
            blocks[c, q] = scores[
                c * count : (c + 1) * count, q * out_width : (q + 1) * out_width
            ]

    def elsewhere(c, q):
        return (c != my_clip) | (my_clip * ratio + q != me)

    @pl.loop(0, nc)
    def _(c):
        @pl.loop(0, ratio)
        def _(q):
            @pl.when(elsewhere(c, q))
            def _():
                block_copy(c, q).start()

            @pl.when(jnp.logical_not(elsewhere(c, q)))
            def _():
                landed_blocks[me] = blocks[c, q]

    holds_own = (me >= my_clip * ratio) & (me < (my_clip + 1) * ratio)

    @pl.loop(0, n)
    def _(z):
        @pl.when((z != me) | jnp.logical_not(holds_own))
        def _():
            wait_for(landed_blocks.at[z], recv_c.at[z])

    total = landed_blocks[0]
    for z in range(1, n):
        total += landed_blocks[z]
    out_ref[...] = total

    other_clips(lambda c: piece_copy(c).wait_send())
    other_clips(lambda c: partial_copy(c).wait_send())

    @pl.loop(0, nc)
    def _(c):
        @pl.loop(0, ratio)
        def _(q):
            @pl.when(elsewhere(c, q))
            def _():
                block_copy(c, q).wait_send()


def on_device(
    nc,
    n,
    clips,
    targets,
    lengths,
    gate_weight,
    up_weight,
    down_weight,
    proj_in,
    proj_out,
    inv_hessian,
    test_sketches,
):
    count, rows, width = clips.shape
    hidden_part = gate_weight.shape[1]
    proj_size = proj_in.shape[0]
    position = jnp.arange(rows, dtype=jnp.int32)
    valid = (position[None, :] < lengths[:, None]).astype(jnp.float32)
    weight = (valid / lengths.astype(jnp.float32)[:, None])[:, :, None]
    start = lax.axis_index("tensor") * width
    proj_cols = lax.dynamic_slice_in_dim(proj_out, start, width, 1)
    pin = jnp.pad(proj_in.T, ((0, 0), (0, proj_size)))
    pout = jnp.pad(proj_cols.T, ((0, 0), (proj_size, 0)))
    both = 2 * proj_size

    tile = 256 if hidden_part % 256 == 0 else hidden_part
    vmem = pl.BlockSpec(memory_space=pltpu.VMEM)
    hbm = pl.BlockSpec(memory_space=pltpu.HBM)
    bf16, f32 = jnp.bfloat16, jnp.float32
    dma = pltpu.SemaphoreType.DMA
    sketches = pl.pallas_call(
        functools.partial(layer_kernel, n, tile),
        out_shape=jax.ShapeDtypeStruct((count, both, both), bf16),
        in_specs=[hbm, vmem, vmem, hbm, hbm, hbm, vmem, vmem],
        out_specs=vmem,
        scratch_shapes=[
            pltpu.VMEM(gate_weight.shape, bf16),
            pltpu.VMEM(up_weight.shape, bf16),
            pltpu.VMEM(down_weight.shape, bf16),
            pltpu.VMEM((count, n, rows, width), bf16),
            pltpu.VMEM((count, n + 1, rows, width), bf16),
            pltpu.VMEM((count, rows, hidden_part), bf16),
            pltpu.VMEM((count, rows, both), f32),
            pltpu.VMEM((n, rows, both), f32),
            pltpu.VMEM((count, both, both), bf16),
            dma((4,)),
            dma((2, count, n)),
            dma((count, n)),
            dma((count, n)),
            dma((count, n + 1)),
            dma((count,)),
            dma((n,)),
            dma((n,)),
            dma((count,)),
        ],
        compiler_params=pltpu.CompilerParams(
            collective_id=0, has_side_effects=True, vmem_limit_bytes=62 * 1024 * 1024
        ),
        cost_estimate=pl.CostEstimate(
            flops=6 * count * rows * hidden_part * width * n,
            bytes_accessed=400_000_000,
            transcendentals=count * rows * hidden_part,
        ),
        name="layer",
    )(clips, targets, weight, gate_weight, up_weight, down_weight, pin, pout)

    flat_sketch = sketches[:, :proj_size, proj_size:].reshape(count, proj_size * proj_size)
    depth, columns = inv_hessian.shape
    tests = test_sketches.shape[0]
    ratio = n // nc
    out_width = tests // ratio
    return pl.pallas_call(
        functools.partial(score_kernel, nc, n),
        out_shape=jax.ShapeDtypeStruct((count, out_width), f32),
        in_specs=[vmem, vmem, vmem],
        out_specs=vmem,
        scratch_shapes=[
            pltpu.VMEM((nc, count, depth), f32),
            pltpu.VMEM((nc, count, depth), f32),
            pltpu.VMEM((nc * count, depth), f32),
            pltpu.VMEM((nc * count, columns), f32),
            pltpu.VMEM((nc, nc * count, columns), f32),
            pltpu.VMEM((nc, ratio, count, out_width), f32),
            pltpu.VMEM((n, count, out_width), f32),
            dma((nc,)),
            dma((nc,)),
            dma((nc,)),
            dma((nc,)),
            dma((nc, ratio)),
            dma((n,)),
        ],
        compiler_params=pltpu.CompilerParams(
            collective_id=1, has_side_effects=True, vmem_limit_bytes=32 * 1024 * 1024
        ),
        name="tail",
    )(flat_sketch, inv_hessian, test_sketches)


def solution(mesh):
    in_specs = (
        P(("parts", "clip"), None, "tensor"),
        P(("parts", "clip"), None, "tensor"),
        P(("parts", "clip")),
        P(None, "tensor"),
        P(None, "tensor"),
        P("tensor", None),
        P(None, "tensor"),
        P(),
        P("clip", "tensor"),
        P("clip", "tensor"),
    )
    out_specs = P(("parts", "clip"), "tensor")
    return jax.shard_map(
        functools.partial(on_device, mesh.shape["clip"], mesh.shape["tensor"]),
        mesh=mesh,
        in_specs=in_specs,
        out_specs=out_specs,
        check_vma=False,
    )
```

```python
import functools

import jax
import jax.numpy as jnp
from jax import lax
from jax.experimental import pallas as pl
from jax.experimental.pallas import tpu as pltpu
from jax.sharding import PartitionSpec as P

MESH = pl.DeviceIdType.MESH


def entry_barrier(n, me):
    barrier = pltpu.get_barrier_semaphore()

    @pl.loop(0, n)
    def _(j):
        @pl.when(j != me)
        def _():
            pl.semaphore_signal(barrier, inc=1, device_id={"tensor": j}, device_id_type=MESH)

    pl.semaphore_wait(barrier, n - 1)


def layer_kernel(
    n,
    tile,
    clips_ref,
    targets_ref,
    lengths_ref,
    gate_hbm,
    up_hbm,
    down_hbm,
    pin_hbm,
    pout_hbm,
    sketch_ref,
    pin_ref,
    pout_ref,
    gate_ref,
    up_ref,
    down_ref,
    tok,
    slots,
    hid,
    joined,
    parts,
    gathered,
    load_sem,
    ag_send,
    ag_recv,
    rs_send,
    rs_recv,
    own_send,
    own_recv,
    sk_send,
    sk_recv,
):
    me = lax.axis_index("tensor")
    count, rows, width = targets_ref.shape
    hidden_part = gate_ref.shape[1]
    proj = pin_hbm.shape[0]
    last = n - 1
    tile_w = 256 if width % 256 == 0 else width

    own = pltpu.make_async_copy(clips_ref, tok.at[:, me], load_sem.at[0])
    own.start()
    loads = [
        pltpu.make_async_copy(gate_hbm, gate_ref, load_sem.at[1]),
        pltpu.make_async_copy(up_hbm, up_ref, load_sem.at[2]),
        pltpu.make_async_copy(down_hbm, down_ref, load_sem.at[3]),
        pltpu.make_async_copy(pin_hbm, pin_ref.at[pl.ds(0, proj)], load_sem.at[4]),
        pltpu.make_async_copy(
            pout_hbm.at[:, pl.ds(pl.multiple_of(me * width, width), width)],
            pout_ref.at[pl.ds(proj, proj)],
            load_sem.at[5],
        ),
    ]
    pin_ref[proj:, :] = jnp.zeros((proj, hidden_part), jnp.bfloat16)
    pout_ref[:proj, :] = jnp.zeros((proj, width), jnp.bfloat16)
    entry_barrier(n, me)
    own.wait()

    def token_copy(side, k, j):
        target = me + 1 if side == 0 else me - 1
        return pltpu.make_async_remote_copy(
            src_ref=tok.at[k, j],
            dst_ref=tok.at[k, j],
            send_sem=ag_send.at[side, k, j],
            recv_sem=ag_recv.at[k, j],
            device_id={"tensor": target},
            device_id_type=MESH,
        )

    def sum_copy(side, k, d):
        if side == 0:
            target, slot = me + 1, d
        else:
            target = me - 1
            slot = jnp.where(d == me - 1, n, d)
        return pltpu.make_async_remote_copy(
            src_ref=slots.at[k, d],
            dst_ref=slots.at[k, slot],
            send_sem=rs_send.at[k, d],
            recv_sem=rs_recv.at[k, slot],
            device_id={"tensor": target},
            device_id_type=MESH,
        )

    def wait_slot(k, slot):
        pltpu.make_async_copy(slots.at[k, slot], slots.at[k, slot], rs_recv.at[k, slot]).wait()

    def wait_token(k, j):
        pltpu.make_async_copy(tok.at[k, j], tok.at[k, j], ag_recv.at[k, j]).wait()

    def partial_tile(k, d, t):
        start = pl.multiple_of(d * width + t * tile_w, tile_w)
        return jnp.dot(
            hid[k], down_ref[:, pl.ds(start, tile_w)], preferred_element_type=jnp.float32
        )

    def add_and_send(side, k, d):
        first = me == (0 if side == 0 else last)

        @pl.when(first)
        def _():
            @pl.loop(0, width // tile_w)
            def _(t):
                cols = pl.ds(pl.multiple_of(t * tile_w, tile_w), tile_w)
                slots[k, d, :, cols] = partial_tile(k, d, t).astype(jnp.bfloat16)

        @pl.when(jnp.logical_not(first))
        def _():
            wait_slot(k, d)

            @pl.loop(0, width // tile_w)
            def _(t):
                cols = pl.ds(pl.multiple_of(t * tile_w, tile_w), tile_w)
                got = slots[k, d, :, cols].astype(jnp.float32)
                slots[k, d, :, cols] = (partial_tile(k, d, t) + got).astype(jnp.bfloat16)

        sum_copy(side, k, d).start()

    def forward_hidden(k):
        @pl.loop(0, hidden_part // tile)
        def _(t):
            cols = pl.ds(pl.multiple_of(t * tile, tile), tile)
            gate_act = jnp.zeros((rows, tile), jnp.float32)
            up_act = jnp.zeros((rows, tile), jnp.float32)
            for j in range(n):
                piece = tok[k, j]
                gate_act += jnp.dot(
                    piece,
                    gate_ref[j * width : (j + 1) * width, cols],
                    preferred_element_type=jnp.float32,
                )
                up_act += jnp.dot(
                    piece,
                    up_ref[j * width : (j + 1) * width, cols],
                    preferred_element_type=jnp.float32,
                )
            silu = gate_act / (1.0 + jnp.exp(-gate_act))
            hid[k, :, cols] = (silu * up_act).astype(jnp.bfloat16)

        joined[k] = lax.dot_general(
            hid[k],
            pin_ref[...],
            (((1,), (1,)), ((), ())),
            preferred_element_type=jnp.float32,
        )

    def finish(k):
        @pl.when(me > 0)
        def _():
            wait_slot(k, me)

        @pl.when(me < last)
        def _():
            wait_slot(k, n)

        from_left = jnp.where(me > 0, 1.0, 0.0)
        from_right = jnp.where(me < last, 1.0, 0.0)
        has_left = jnp.full((rows, tile_w), from_left, jnp.float32) > 0.5
        has_right = jnp.full((rows, tile_w), from_right, jnp.float32) > 0.5
        length = jnp.full((rows, tile_w), lengths_ref[k], jnp.int32)
        position = lax.broadcasted_iota(jnp.int32, (rows, tile_w), 0)
        weight = jnp.where(position < length, 1.0 / length.astype(jnp.float32), 0.0)

        @pl.loop(0, width // tile_w)
        def _(t):
            cols = pl.ds(pl.multiple_of(t * tile_w, tile_w), tile_w)
            total = partial_tile(k, me, t)
            total += jnp.where(has_left, slots[k, me, :, cols].astype(jnp.float32), 0.0)
            total += jnp.where(has_right, slots[k, n, :, cols].astype(jnp.float32), 0.0)
            differ = jnp.clip(total - targets_ref[k, :, cols].astype(jnp.float32), -1.0, 1.0)
            grad = (differ * weight).astype(jnp.bfloat16)
            joined[k] += lax.dot_general(
                grad,
                pout_ref[:, cols],
                (((1,), (1,)), ((), ())),
                preferred_element_type=jnp.float32,
            )

        @pl.when(me != k)
        def _():
            part_copy(k).start()

    def part_copy(k):
        return pltpu.make_async_remote_copy(
            src_ref=joined.at[k],
            dst_ref=parts.at[me],
            send_sem=own_send.at[k],
            recv_sem=own_recv.at[me],
            device_id={"tensor": k},
            device_id_type=MESH,
        )

    def sketch_copy(j):
        return pltpu.make_async_remote_copy(
            src_ref=gathered.at[me],
            dst_ref=gathered.at[me],
            send_sem=sk_send.at[j],
            recv_sem=sk_recv.at[me],
            device_id={"tensor": j},
            device_id_type=MESH,
        )

    @pl.loop(0, count + 2 * last)
    def _(step):
        @pl.when(step < count)
        def _():
            @pl.when(me < last)
            def _():
                token_copy(0, step, me).start()

            @pl.when(me > 0)
            def _():
                token_copy(1, step, me).start()

        @pl.when(step == 0)
        def _():
            for load in loads:
                load.start()

        @pl.loop(1, n)
        def _(h):
            k = step - h

            @pl.when((k >= 0) & (k < count))
            def _():
                @pl.when(me - h >= 0)
                def _():
                    wait_token(k, me - h)

                    @pl.when(me < last)
                    def _():
                        token_copy(0, k, me - h).start()

                @pl.when(me + h <= last)
                def _():
                    wait_token(k, me + h)

                    @pl.when(me > 0)
                    def _():
                        token_copy(1, k, me + h).start()

        @pl.when(step == last)
        def _():
            for load in loads:
                load.wait()

        k_now = step - last

        @pl.when((k_now >= 0) & (k_now < count))
        def _():
            forward_hidden(k_now)

        k_right = step - last - me

        @pl.when((k_right >= 0) & (k_right < count))
        def _():
            @pl.loop(0, last - me)
            def _(i):
                add_and_send(0, k_right, last - i)

        k_left = step - last - (last - me)

        @pl.when((k_left >= 0) & (k_left < count))
        def _():
            @pl.loop(0, me)
            def _(d):
                add_and_send(1, k_left, d)

        k_end = step - 2 * last

        @pl.when((k_end >= 0) & (k_end < count))
        def _():
            finish(k_end)

    @pl.when(me < count)
    def _():
        total = joined[me]
        parts[me] = total

        @pl.loop(0, n)
        def _(j):
            @pl.when(j != me)
            def _():
                pltpu.make_async_copy(parts.at[j], parts.at[j], own_recv.at[j]).wait()

        total = parts[0]
        for j in range(1, n):
            total += parts[j]
        product = jnp.dot(
            total.T,
            total,
            precision=lax.Precision.HIGHEST,
            preferred_element_type=jnp.float32,
        )
        gathered[me] = product.astype(jnp.bfloat16)

        @pl.loop(0, n)
        def _(j):
            @pl.when(j != me)
            def _():
                sketch_copy(j).start()

    @pl.loop(0, count)
    def _(k):
        @pl.when(k != me)
        def _():
            pltpu.make_async_copy(gathered.at[k], gathered.at[k], sk_recv.at[k]).wait()

    sketch_ref[...] = gathered[...]

    @pl.when(me < count)
    def _():
        @pl.loop(0, n)
        def _(j):
            @pl.when(j != me)
            def _():
                sketch_copy(j).wait_send()

    @pl.loop(0, count)
    def _(k):
        @pl.when(k != me)
        def _():
            part_copy(k).wait_send()

        @pl.loop(0, n)
        def _(j):
            @pl.when((j <= me) & (me < last))
            def _():
                token_copy(0, k, j).wait_send()

            @pl.when((j >= me) & (me > 0))
            def _():
                token_copy(1, k, j).wait_send()

            @pl.when(j > me)
            def _():
                sum_copy(0, k, j).wait_send()

            @pl.when(j < me)
            def _():
                sum_copy(1, k, j).wait_send()


def score_kernel(
    nc,
    n,
    flat_ref,
    hessian_hbm,
    tests_hbm,
    out_ref,
    hessian_ref,
    tests_ref,
    load_sem,
    pieces,
    landed_pieces,
    stacked,
    partial,
    landed_partial,
    blocks,
    landed_blocks,
    send_a,
    recv_a,
    send_b,
    recv_b,
    send_c,
    recv_c,
):
    my_clip = lax.axis_index("clip")
    me = lax.axis_index("tensor")
    count, out_width = out_ref.shape
    depth = hessian_ref.shape[0]
    ratio = n // nc

    load_hessian = pltpu.make_async_copy(hessian_hbm, hessian_ref, load_sem.at[0])
    load_tests = pltpu.make_async_copy(tests_hbm, tests_ref, load_sem.at[1])
    load_hessian.start()
    load_tests.start()
    barrier = pltpu.get_barrier_semaphore()

    @pl.loop(0, nc)
    def _(c):
        @pl.loop(0, n)
        def _(z):
            @pl.when((c != my_clip) | (z != me))
            def _():
                pl.semaphore_signal(
                    barrier, inc=1, device_id={"clip": c, "tensor": z}, device_id_type=MESH
                )

    for c in range(nc):
        pieces[c] = flat_ref[:, c * depth : (c + 1) * depth].astype(jnp.float32)
    pl.semaphore_wait(barrier, nc * n - 1)

    def piece_copy(c):
        return pltpu.make_async_remote_copy(
            src_ref=pieces.at[c],
            dst_ref=landed_pieces.at[my_clip],
            send_sem=send_a.at[c],
            recv_sem=recv_a.at[my_clip],
            device_id={"clip": c, "tensor": me},
            device_id_type=MESH,
        )

    def partial_copy(c):
        return pltpu.make_async_remote_copy(
            src_ref=partial,
            dst_ref=landed_partial.at[my_clip],
            send_sem=send_b.at[c],
            recv_sem=recv_b.at[my_clip],
            device_id={"clip": c, "tensor": me},
            device_id_type=MESH,
        )

    def block_copy(c, q):
        return pltpu.make_async_remote_copy(
            src_ref=blocks.at[c, q],
            dst_ref=landed_blocks.at[me],
            send_sem=send_c.at[c, q],
            recv_sem=recv_c.at[me],
            device_id={"clip": c, "tensor": my_clip * ratio + q},
            device_id_type=MESH,
        )

    def other_clips(act):
        @pl.loop(0, nc)
        def _(c):
            @pl.when(c != my_clip)
            def _():
                act(c)

    def wait_for(ref, sem):
        pltpu.make_async_copy(ref, ref, sem).wait()

    other_clips(lambda c: piece_copy(c).start())
    landed_pieces[my_clip] = pieces[my_clip]
    other_clips(lambda c: wait_for(landed_pieces.at[c], recv_a.at[c]))
    for c in range(nc):
        stacked[c * count : (c + 1) * count, :] = landed_pieces[c]
    load_hessian.wait()
    partial[...] = jnp.dot(
        stacked[...].astype(jnp.bfloat16),
        hessian_ref[...],
        preferred_element_type=jnp.float32,
    )
    other_clips(lambda c: partial_copy(c).start())
    landed_partial[my_clip] = partial[...]
    other_clips(lambda c: wait_for(landed_partial.at[c], recv_b.at[c]))
    load_tests.wait()
    precond = landed_partial[0]
    for c in range(1, nc):
        precond += landed_partial[c]
    scores = lax.dot_general(
        precond.astype(jnp.bfloat16),
        tests_ref[...],
        (((1,), (1,)), ((), ())),
        preferred_element_type=jnp.float32,
    )
    for c in range(nc):
        for q in range(ratio):
            blocks[c, q] = scores[
                c * count : (c + 1) * count, q * out_width : (q + 1) * out_width
            ]

    def elsewhere(c, q):
        return (c != my_clip) | (my_clip * ratio + q != me)

    @pl.loop(0, nc)
    def _(c):
        @pl.loop(0, ratio)
        def _(q):
            @pl.when(elsewhere(c, q))
            def _():
                block_copy(c, q).start()

            @pl.when(jnp.logical_not(elsewhere(c, q)))
            def _():
                landed_blocks[me] = blocks[c, q]

    holds_own = (me >= my_clip * ratio) & (me < (my_clip + 1) * ratio)

    @pl.loop(0, n)
    def _(z):
        @pl.when((z != me) | jnp.logical_not(holds_own))
        def _():
            wait_for(landed_blocks.at[z], recv_c.at[z])

    total = landed_blocks[0]
    for z in range(1, n):
        total += landed_blocks[z]
    out_ref[...] = total

    other_clips(lambda c: piece_copy(c).wait_send())
    other_clips(lambda c: partial_copy(c).wait_send())

    @pl.loop(0, nc)
    def _(c):
        @pl.loop(0, ratio)
        def _(q):
            @pl.when(elsewhere(c, q))
            def _():
                block_copy(c, q).wait_send()


def on_device(
    nc,
    n,
    clips,
    targets,
    lengths,
    gate_weight,
    up_weight,
    down_weight,
    proj_in,
    proj_out,
    inv_hessian,
    test_sketches,
):
    count, rows, width = clips.shape
    hidden_part = gate_weight.shape[1]
    proj_size = proj_in.shape[0]
    both = 2 * proj_size

    tile = 256 if hidden_part % 256 == 0 else hidden_part
    vmem = pl.BlockSpec(memory_space=pltpu.VMEM)
    hbm = pl.BlockSpec(memory_space=pltpu.HBM)
    smem = pl.BlockSpec(memory_space=pltpu.SMEM)
    bf16, f32 = jnp.bfloat16, jnp.float32
    dma = pltpu.SemaphoreType.DMA
    sketches = pl.pallas_call(
        functools.partial(layer_kernel, n, tile),
        out_shape=jax.ShapeDtypeStruct((count, both, both), bf16),
        in_specs=[hbm, vmem, smem, hbm, hbm, hbm, hbm, hbm],
        out_specs=vmem,
        scratch_shapes=[
            pltpu.VMEM((both, hidden_part), bf16),
            pltpu.VMEM((both, width), bf16),
            pltpu.VMEM(gate_weight.shape, bf16),
            pltpu.VMEM(up_weight.shape, bf16),
            pltpu.VMEM(down_weight.shape, bf16),
            pltpu.VMEM((count, n, rows, width), bf16),
            pltpu.VMEM((count, n + 1, rows, width), bf16),
            pltpu.VMEM((count, rows, hidden_part), bf16),
            pltpu.VMEM((count, rows, both), f32),
            pltpu.VMEM((n, rows, both), f32),
            pltpu.VMEM((count, both, both), bf16),
            dma((6,)),
            dma((2, count, n)),
            dma((count, n)),
            dma((count, n)),
            dma((count, n + 1)),
            dma((count,)),
            dma((n,)),
            dma((n,)),
            dma((count,)),
        ],
        compiler_params=pltpu.CompilerParams(
            collective_id=0, has_side_effects=True, vmem_limit_bytes=62 * 1024 * 1024
        ),
        cost_estimate=pl.CostEstimate(
            flops=6 * count * rows * hidden_part * width * n,
            bytes_accessed=400_000_000,
            transcendentals=count * rows * hidden_part,
        ),
        name="layer",
    )(clips, targets, lengths, gate_weight, up_weight, down_weight, proj_in, proj_out)

    flat_sketch = sketches[:, :proj_size, proj_size:].reshape(count, proj_size * proj_size)
    depth, columns = inv_hessian.shape
    tests = test_sketches.shape[0]
    ratio = n // nc
    out_width = tests // ratio
    return pl.pallas_call(
        functools.partial(score_kernel, nc, n),
        out_shape=jax.ShapeDtypeStruct((count, out_width), f32),
        in_specs=[vmem, hbm, hbm],
        out_specs=vmem,
        scratch_shapes=[
            pltpu.VMEM((depth, columns), bf16),
            pltpu.VMEM(test_sketches.shape, bf16),
            dma((2,)),
            pltpu.VMEM((nc, count, depth), f32),
            pltpu.VMEM((nc, count, depth), f32),
            pltpu.VMEM((nc * count, depth), f32),
            pltpu.VMEM((nc * count, columns), f32),
            pltpu.VMEM((nc, nc * count, columns), f32),
            pltpu.VMEM((nc, ratio, count, out_width), f32),
            pltpu.VMEM((n, count, out_width), f32),
            dma((nc,)),
            dma((nc,)),
            dma((nc,)),
            dma((nc,)),
            dma((nc, ratio)),
            dma((n,)),
        ],
        compiler_params=pltpu.CompilerParams(
            collective_id=1, has_side_effects=True, vmem_limit_bytes=32 * 1024 * 1024
        ),
        name="tail",
    )(flat_sketch, inv_hessian, test_sketches)


def solution(mesh):
    in_specs = (
        P(("parts", "clip"), None, "tensor"),
        P(("parts", "clip"), None, "tensor"),
        P(("parts", "clip")),
        P(None, "tensor"),
        P(None, "tensor"),
        P("tensor", None),
        P(None, "tensor"),
        P(),
        P("clip", "tensor"),
        P("clip", "tensor"),
    )
    out_specs = P(("parts", "clip"), "tensor")
    return jax.shard_map(
        functools.partial(on_device, mesh.shape["clip"], mesh.shape["tensor"]),
        mesh=mesh,
        in_specs=in_specs,
        out_specs=out_specs,
        check_vma=False,
    )
```
